32 devices in a mesh: groups: 2 (over y), samp: 4 (over z), feat: 4 (over x, core).
Axes of the slice: x: 2, y: 2, z: 4, core: 2. Of those that a mesh axis runs over, the one named last changes fastest.
Arguments:
- x_blocks: bfloat16 [64, 64, 128, 128], P(('groups', 'samp'), 'feat'), parts along dimension 0, may hold values from -6 to 6
- block_cols: int32 [64, 64], P('groups', 'feat'), parts along dimension 0, may hold values from 0 to 31
- labels: int32 [8192], P('groups'), parts along dimension 0, may hold values from 0 to 63
- group_ids: int32 [8192], P('groups'), parts along dimension 0, may hold values from 0 to 7, as said below
- picks: int32 [3, 32], P(None, 'groups'), parts along dimension 1, may hold values from 0 to 31, as said below
- w_init: float32 [16384, 64], P('feat'), may hold values from -2.253903 to 2.253903
Outputs:
- scores: float32 [8192, 64], P(('groups', 'samp')), parts along dimension 0
- adversary: float32 [16], P('groups'), parts along dimension 0
The draws below stay inside these ranges and needn't reach their ends.
There are 2 independent parts, one for each index of `groups`. The reference program is written for one: setup_inputs(seed, part) draws one part's arguments, and reference() takes and returns one part's arrays. A program takes and returns all parts, laid end to end along the dimension named above; an argument that names none is the same for every part. Nothing has to cross between parts.
Inputs may be any that keep to these rules, and one draw needn't show every extreme that they name: `group_ids`: every row block of 128 samples holds every group at least once. `picks`: the entries of one step are distinct. Row block b is owned by index b // 8 of samp. The k-th aligned block of 4 entries of a step is the list of index k of samp; it names row blocks owned by index k or by the next index along samp (index 0 after the last); between one and 2 entries of each list name the next index's row blocks, exactly 2 in at least one list of every step.
All inputs are finite; a program needn't handle non-finite values.
Results may differ from the reference program's by a relative error of at most 0.00315.
The reference program's roundings to bfloat16 on the way count: a program that leaves them out, or rounds other values in their place, can miss the bound.
Values may be sent and summed in bfloat16 or wider, within the bound.
No kernel may reach another device: no remote copies, remote signals or barrier semaphores. Data moves between devices by JAX's collectives and lax.ppermute only.
A program may use at most 64 MiB of HBM per device.

```python
import jax
import jax.numpy as jnp
from jax import lax

BLK = 128
C = 64
GRP = 8
BPR = 16
STEPS = 3
RB_DEV = 8
SEL_DEV = 4
LEND = 2
NRB = 32
ROWS = 4096
NBLK = 64
CB = 32
FEAT = 16384
SEL = 16
N_SAMP = 4
N_FEAT = 4


def draw_w_init(key, part):
    first_key = jax.random.fold_in(jax.random.fold_in(key, 17), 0)
    scale = 3.0 / jnp.sqrt(jnp.float32(NBLK * BLK))
    values = jnp.clip(jax.random.normal(first_key, (FEAT, C), jnp.float32), -6.0, 6.0)
    return (values * scale).astype(jnp.float32)


def draw_group_ids(key, part):
    first_key, second_key = jax.random.split(jax.random.fold_in(key, 41))
    free_ids = jax.random.randint(first_key, (NRB, BLK), 0, GRP).astype(jnp.int32)
    ranks = jax.vmap(lambda single: jax.random.permutation(single, BLK))(jax.random.split(second_key, NRB)).astype(jnp.int32)
    chosen = jnp.where(ranks < GRP, ranks, free_ids)
    return chosen.reshape(-1).astype(jnp.int32)


def draw_picks(key, part):
    start_key = jax.random.fold_in(key, 29)
    device_range = jnp.arange(N_SAMP, dtype=jnp.int32)
    next_device = (device_range + 1) % N_SAMP
    slot_range = jnp.arange(SEL_DEV, dtype=jnp.int32)
    all_lists = []
    for step in range(STEPS):
        step_keys = jax.random.split(jax.random.fold_in(start_key, step), 4)
        borrow = jax.random.randint(step_keys[0], (N_SAMP,), 1, LEND + 1).astype(jnp.int32)
        forced = jax.random.randint(step_keys[1], (), 0, N_SAMP).astype(jnp.int32)
        borrow = jnp.where(device_range == forced, LEND, borrow).astype(jnp.int32)
        own_count = (SEL_DEV - borrow).astype(jnp.int32)
        orders = jax.vmap(lambda single: jax.random.permutation(single, RB_DEV))(jax.random.split(step_keys[2], N_SAMP)).astype(jnp.int32)
        next_place = jnp.clip(own_count[next_device][:, None] + slot_range[None, :] - own_count[:, None], 0, RB_DEV - 1)
        next_local = jnp.take_along_axis(orders[next_device], next_place, axis=1)
        own_local = orders[:, :SEL_DEV]
        entries = jnp.where(slot_range[None, :] < own_count[:, None], device_range[:, None] * RB_DEV + own_local, next_device[:, None] * RB_DEV + next_local)
        shuffle = jax.vmap(lambda single: jax.random.permutation(single, SEL_DEV))(jax.random.split(step_keys[3], N_SAMP)).astype(jnp.int32)
        entries = jnp.take_along_axis(entries, shuffle, axis=1)
        all_lists.append(entries.reshape(-1).astype(jnp.int32))
    return jnp.stack(all_lists).astype(jnp.int32)


def plant(values, stream_key, low, high):
    index_at = [jax.random.randint(jax.random.fold_in(stream_key, axis), (), 0, length) for axis, length in enumerate(values.shape)]
    widest = values.shape.index(max(values.shape))
    beside = index_at[:widest] + [(index_at[widest] + 1) % values.shape[widest]] + index_at[widest + 1:]
    return values.at[tuple(index_at)].set(low).at[tuple(beside)].set(high)


def shard_levels(rng, extent, shards, smallest, high):
    gain, own = 1.0, jax.random.fold_in(rng, 6)
    for position, blocks in shards:
        draws = jnp.exp(jax.random.uniform(jax.random.fold_in(own, position), (blocks,), jnp.float32, smallest / len(shards), high / len(shards)))
        gain = gain * jnp.repeat(draws, extent[position] // blocks).reshape([-1 if axis == position else 1 for axis in range(len(extent))])
    return gain


def bell_draw(stream_key, dims, width, most, cuts=(), held_as=jnp.bfloat16):
    array = width * jax.random.normal(stream_key, dims, jnp.float32)
    if cuts:
        array = array * shard_levels(stream_key, dims, cuts, -0.22, 0.18)
    return jnp.clip(array, -most, most).astype(held_as)


def setup_inputs(seed: int = 0, part: int = 0) -> dict:
    splits = jax.random.split(jax.random.key(seed), 7)
    own_keys = jax.random.split(jax.random.fold_in(splits[6], part), 7)
    return {
        "x_blocks": bell_draw(own_keys[0], (NRB, NBLK, BLK, BLK), 1.0, 6.0, ((0, 4), (1, 4))),
        "block_cols": plant(jax.random.randint(own_keys[1], (NRB, NBLK), 0, CB), jax.random.fold_in(own_keys[1], 1), 0, CB - 1).astype(jnp.int32),
        "labels": plant(jax.random.randint(own_keys[2], (ROWS,), 0, C), jax.random.fold_in(own_keys[2], 1), 0, C - 1).astype(jnp.int32),
        "group_ids": draw_group_ids(jax.random.fold_in(jax.random.fold_in(splits[6], part), 71), part),
        "picks": draw_picks(jax.random.fold_in(jax.random.fold_in(splits[6], part), 71), part),
        "w_init": draw_w_init(jax.random.fold_in(splits[6], 71), part),
    }


weight_rate = 8.0
adv_rate = 2.0


def reference(x_blocks, block_cols, labels, group_ids, picks, w_init):
    col_offsets = (jnp.arange(NBLK, dtype=jnp.int32) // BPR) * CB
    global_cols = (block_cols + col_offsets[None, :]).astype(jnp.int32)
    label_hot = (labels[:, None] == jnp.arange(C, dtype=jnp.int32)[None, :]).astype(jnp.float32)
    group_hot = (group_ids[:, None] == jnp.arange(GRP, dtype=jnp.int32)[None, :]).astype(jnp.float32)
    step_rate = weight_rate * SEL / (BPR * N_FEAT)
    block_index = jnp.arange(NRB, dtype=jnp.int32)

    def scores(weights_bf):
        tiles_all = weights_bf.reshape(FEAT // BLK, BLK, C)

        def one_block(pair):
            x_row, col_row = pair
            tiles = tiles_all[col_row]
            return jnp.einsum("bij,bjc->ic", x_row.astype(jnp.float32), tiles.astype(jnp.float32))

        return lax.map(one_block, (x_blocks, global_cols)).reshape(ROWS, C)

    def gradient(dz_blocks):
        def add_block(total, triple):
            x_row, col_row, dz_row = triple
            piece = jnp.einsum("bij,ic->bjc", x_row.astype(jnp.float32), dz_row.astype(jnp.float32))
            return total.at[col_row].add(piece), None

        start = jnp.zeros((FEAT // BLK, BLK, C), jnp.float32)
        total, _ = lax.scan(add_block, start, (x_blocks, global_cols, dz_blocks))
        return total.reshape(FEAT, C)

    def evaluate(weights_bf, adversary, mult_rows, counts):
        logits = scores(weights_bf)
        log_total = jax.nn.logsumexp(logits, axis=-1)
        cross = log_total - jnp.sum(logits * label_hot, axis=-1)
        probs = jnp.exp(logits - log_total[:, None])
        loss = jnp.dot(mult_rows * cross, group_hot, precision=lax.Precision.HIGHEST) / counts
        coef = jnp.dot(group_hot, adversary / counts, precision=lax.Precision.HIGHEST) * mult_rows
        dz_rows = (coef[:, None] * (probs - label_hot)).astype(jnp.bfloat16)
        return loss, gradient(dz_rows.reshape(NRB, BLK, C))

    weights = w_init
    adversary = jnp.full((GRP,), 1.0 / GRP, jnp.float32)
    for step in range(STEPS):
        hits = jnp.sum((picks[step][None, :] == block_index[:, None]).astype(jnp.float32), axis=1)
        mult_rows = jnp.repeat(hits, BLK)
        counts = jnp.dot(mult_rows, group_hot, precision=lax.Precision.HIGHEST)
        loss_first, grad_first = evaluate(weights.astype(jnp.bfloat16), adversary, mult_rows, counts)
        half_weights = weights - step_rate * grad_first
        half_adv = jax.nn.softmax(jnp.log(adversary) + adv_rate * loss_first)
        loss_second, grad_second = evaluate(half_weights.astype(jnp.bfloat16), half_adv, mult_rows, counts)
        weights = weights - step_rate * grad_second
        adversary = jax.nn.softmax(jnp.log(adversary) + adv_rate * loss_second)
    return (scores(weights.astype(jnp.bfloat16)), adversary)
```

```python
import functools

import jax
import jax.numpy as jnp
from jax import lax
from jax.experimental import pallas as pl
from jax.experimental.pallas import tpu as pltpu
from jax.sharding import PartitionSpec as P

GRP = 8
STEPS = 3
LEND = 2
LANES = 128
CUTS = (64,)

weight_rate = 8.0
adv_rate = 2.0

F32 = jnp.float32
BF16 = jnp.bfloat16
VM = pl.BlockSpec(memory_space=pltpu.VMEM)
SM = pl.BlockSpec(memory_space=pltpu.SMEM)
HBM = pl.BlockSpec(memory_space=pltpu.HBM)
PARAMS = pltpu.CompilerParams(vmem_limit_bytes=24 << 20)


def shape(dims, dtype):
    return jax.ShapeDtypeStruct(dims, dtype)


def cost(flops, bytes_accessed):
    return pl.CostEstimate(flops=flops, bytes_accessed=bytes_accessed, transcendentals=0)


def lane_sum(rows):
    return jnp.broadcast_to(jnp.sum(rows, axis=1, keepdims=True), rows.shape)


def tree_sum(parts):
    while len(parts) > 1:
        parts = [a + b for a, b in zip(parts[::2], parts[1::2], strict=True)]
    return parts[0]


def group_hot(row):
    return (lax.broadcasted_iota(jnp.int32, (GRP, LANES), 0) == row).astype(F32)


def row_data(x_ref, row):
    return jnp.concatenate([x_ref[row, j] for j in range(x_ref.shape[1])], axis=1)


def setup_kernel(
    sel, row_blocks, bounds, me_ref, picks_hbm, cols_hbm, gid_hbm, w_hbm, x_hbm, slots_ref, live_ref, counts_ref, xv_ref,
    *refs
):
    chunks = len(bounds)
    owns, zs = refs[:chunks], refs[chunks : 2 * chunks]
    wall, picks_ref, cols_ref, gid_ref, w_ref, sems = refs[2 * chunks :]

    def fetch(source, target, place):
        copy = pltpu.make_async_copy(source, target, sems.at[place])
        copy.start()
        return copy

    get_picks = fetch(picks_hbm, picks_ref, 0)
    get_w = fetch(w_hbm, w_ref, 1)
    get_cols = fetch(cols_hbm, cols_ref, 2)
    get_gid = fetch(gid_hbm, gid_ref, 3)
    get_rows = [fetch(x_hbm.at[row], xv_ref.at[row], 4 + row) for row in range(row_blocks)]
    slots = slots_ref.shape[1]
    me = me_ref[0]
    samp_count = picks_ref.shape[1] // sel
    before = lax.rem(me + samp_count - 1, samp_count)
    for step in range(STEPS):
        for slot in range(slots):
            slots_ref[step, slot] = 0
            live_ref[step, slot] = 0
    get_picks.wait()
    for step in range(STEPS):
        found = jnp.int32(0)
        for start in (me * sel, before * sel):
            for entry in range(sel):
                block = picks_ref[step, start + entry]
                mine = (block // row_blocks) == me
                place = jnp.minimum(found, slots - 1)

                @pl.when(mine)
                def _(step=step, place=place, block=block):
                    slots_ref[step, place] = block - me * row_blocks
                    live_ref[step, place] = 1

                found = found + mine.astype(jnp.int32)
    get_w.wait()
    for col in range(wall.shape[0]):
        wall[col] = w_ref[:, col * LANES : (col + 1) * LANES].astype(BF16)
    size = owns[0].shape[0]
    for col in range(size):
        start = pl.multiple_of((me * size + col) * LANES, LANES)
        for own, (low, high) in zip(owns, bounds, strict=True):
            own[col] = w_ref[low:high, pl.ds(start, LANES)]
    get_gid.wait()
    for step in range(STEPS):

        def count(entry, total, step=step):
            return total + group_hot(gid_ref[pl.ds(picks_ref[step, entry], 1), :])

        total = lax.fori_loop(0, picks_ref.shape[1], count, jnp.zeros((GRP, LANES), F32))
        counts_ref[step] = lane_sum(total)
    get_cols.wait()
    for copy in get_rows:
        copy.wait()
    for slot in range(slots):
        row = slots_ref[0, slot]
        tiles = jnp.concatenate([wall[cols_ref[j, me * row_blocks + row]] for j in range(xv_ref.shape[1])], axis=1)
        piece = lax.dot_general(
            tiles, row_data(xv_ref, row), (((1,), (1,)), ((), ())), preferred_element_type=F32
        )
        for z, (low, high) in zip(zs, bounds, strict=True):
            z[slot] = piece[low:high]


def flip_kernel(x_ref, out_ref):
    for row in range(x_ref.shape[0]):
        for j in range(x_ref.shape[1]):
            out_ref[row, j] = x_ref[row, j].T


def forward_kernel(step, row_blocks, me_ref, slots_ref, cols_ref, xt_ref, *refs):
    parts, (z_ref, wall) = refs[:-2], refs[-2:]
    me = me_ref[0]
    per_row, depth, rows = xt_ref.shape[1:]
    if len(parts) > 1:
        size = parts[0].shape[0]
        for mask in range(len(parts)):
            start = (me ^ mask) * size
            for col in range(size):
                wall[start + col] = parts[mask][col]
        weights = wall
    else:
        weights = parts[0]
    for slot in range(z_ref.shape[0]):
        row = slot if step is None else slots_ref[step, slot]
        tiles = jnp.concatenate([weights[cols_ref[j, me * row_blocks + row]] for j in range(per_row)], axis=1)
        z_ref[slot] = jnp.dot(tiles, xt_ref[row].reshape(per_row * depth, rows), preferred_element_type=F32)


def send_out(n_samp, me, acc, own_ref, sends, tail):
    size, classes, _ = own_ref.shape
    rows = size * classes
    for col in range(size):
        own_ref[col] = acc[me * size + col]
    if len(sends) == 1:
        for owner in range(n_samp):
            for col in range(size):
                sends[0][owner, col * classes : (col + 1) * classes, :] = acc[owner * size + col].astype(
                    sends[0].dtype
                )
            if tail is not None:
                sends[0][owner, rows : rows + tail.shape[0], :] = tail
        return
    for mask in range(1, n_samp):
        send = sends[mask - 1]
        start = (me ^ mask) * size
        for col in range(size):
            send[col * classes : (col + 1) * classes, :] = acc[start + col].astype(send.dtype)
        if tail is not None:
            send[rows : rows + tail.shape[0], :] = tail


def add_pieces(acc, cols_ref, row, piece):
    for j in range(cols_ref.shape[0]):
        col = cols_ref[j, row]
        acc[col] = acc[col] + piece[:, j * LANES : (j + 1) * LANES]


def grad_kernel(
    step, n_samp, row_blocks, bounds, me_ref, slots_ref, live_ref, cols_ref, x_ref, label_ref, gid_ref, q_ref, counts_ref,
    *refs
):
    chunks = len(bounds)
    halves, refs = refs[: 2 * chunks], refs[2 * chunks :]
    (own_ref, loss_ref), rests, refs = refs[:2], refs[2 : 1 + chunks], refs[1 + chunks :]
    sends, acc = refs[:-1], refs[-1]
    me = me_ref[0]
    acc[...] = jnp.zeros_like(acc)
    classes = bounds[-1][1]
    weight = q_ref[...] / counts_ref[step]
    loss = jnp.zeros((GRP, LANES), F32)
    for slot in range(slots_ref.shape[1]):
        local = slots_ref[step, slot]
        row = me * row_blocks + local
        mult = live_ref[step, slot].astype(F32)
        logits = jnp.concatenate([halves[2 * h][slot] + halves[2 * h + 1][slot] for h in range(chunks)], axis=0)
        hot = (
            lax.broadcasted_iota(jnp.int32, (classes, LANES), 0) == label_ref[pl.ds(row, 1), :]
        ).astype(F32)
        groups = group_hot(gid_ref[pl.ds(row, 1), :])
        top = jnp.max(logits, axis=0, keepdims=True)
        log_total = top + jnp.log(jnp.sum(jnp.exp(logits - top), axis=0, keepdims=True))
        cross = log_total - jnp.sum(logits * hot, axis=0, keepdims=True)
        probs = jnp.exp(logits - log_total)
        loss = loss + groups * (mult * cross)
        coef = jnp.sum(groups * weight, axis=0, keepdims=True) * mult
        dz = (coef * (probs - hot)).astype(BF16)
        for rest, (low, high) in zip(rests, bounds[1:], strict=True):
            rest[slot] = dz[low:high]
        piece = jnp.dot(dz[: bounds[0][1]], row_data(x_ref, local), preferred_element_type=F32)
        add_pieces(acc, cols_ref, row, piece)
    loss = lane_sum(loss)
    loss_ref[...] = loss
    tail = loss
    if sends[0].dtype == BF16:
        high = loss.astype(BF16).astype(F32)
        rest = loss - high
        middle = rest.astype(BF16).astype(F32)
        low = rest - middle
        left = lax.broadcasted_iota(jnp.int32, (GRP, LANES), 1) < LANES // 2
        tail = jnp.concatenate([jnp.where(left, high, low), middle], axis=0).astype(BF16)
    send_out(n_samp, me, acc, own_ref, sends, tail)


def more_grad_kernel(step, n_samp, row_blocks, me_ref, slots_ref, cols_ref, x_ref, dz_ref, own_ref, *refs):
    sends, acc = refs[:-1], refs[-1]
    me = me_ref[0]
    acc[...] = jnp.zeros_like(acc)
    for slot in range(slots_ref.shape[1]):
        local = slots_ref[step, slot]
        piece = jnp.dot(dz_ref[slot], row_data(x_ref, local), preferred_element_type=F32)
        add_pieces(acc, cols_ref, me * row_blocks + local, piece)
    send_out(n_samp, me, acc, own_ref, sends, None)


def new_weights(rate, me_ref, own_ref, w_ref, recvs, w_out, wbf_out):
    size, classes, _ = own_ref.shape
    for col in range(size):
        span = slice(col * classes, (col + 1) * classes)
        own = own_ref[col]
        if len(recvs) == 1:
            parts = [
                jnp.where(me_ref[0] == i, own, recvs[0][i, span, :].astype(F32)) for i in range(recvs[0].shape[0])
            ]
        else:
            parts = [own] + [recv[span, :].astype(F32) for recv in recvs]
        state = w_ref[col] - rate * tree_sum(parts)
        if w_out is not None:
            w_out[col] = state
        wbf_out[col] = state.astype(BF16)


def update_kernel(step, rate, keep, count, me_ref, own_ref, w_ref, loss_ref, q_ref, counts_ref, *refs):
    recvs, outs = list(refs[:count])[::-1], list(refs[count:])
    size, classes, _ = own_ref.shape
    rows = size * classes
    more = 2 * GRP if recvs[0].dtype == BF16 else GRP

    def loss_of(tail):
        if tail.dtype == F32:
            return tail[:, :1]
        tail = tail.astype(F32)
        return (tail[:GRP, :1] + tail[GRP:, :1]) + tail[:GRP, LANES // 2 : LANES // 2 + 1]

    if len(recvs) == 1:
        loss = tree_sum([loss_of(recvs[0][i, rows : rows + more, :]) for i in range(recvs[0].shape[0])])
    else:
        loss = tree_sum([loss_ref[:, :1]] + [loss_of(recv[rows : rows + more, :]) for recv in recvs])
    score = jnp.log(q_ref[...]) + adv_rate * (loss / counts_ref[step])
    grown = jnp.exp(score - jnp.max(score, axis=0, keepdims=True))
    outs[0][...] = grown / jnp.sum(grown, axis=0, keepdims=True)
    new_weights(rate, me_ref, own_ref, w_ref, recvs, outs[2] if keep else None, outs[1])


def more_update_kernel(rate, keep, count, me_ref, own_ref, w_ref, *refs):
    recvs, outs = list(refs[:count])[::-1], list(refs[count:])
    new_weights(rate, me_ref, own_ref, w_ref, recvs, outs[1] if keep else None, outs[0])


def scores_kernel(bounds, *refs):
    out_ref = refs[-1]
    for h, (low, high) in enumerate(bounds):
        for block in range(refs[0].shape[0]):
            out_ref[low:high, block * LANES : (block + 1) * LANES] = refs[2 * h][block] + refs[2 * h + 1][block]


def swap(value, axis, mask):
    count = lax.axis_size(axis)
    return lax.ppermute(value, axis, [(i, i ^ mask) for i in range(count)])


def swaps(values, axis):
    count = len(values) + 1
    order = sorted(range(1, count), key=lambda mask: (mask < count // 2, mask))
    got = {mask: swap(values[mask - 1], axis, mask) for mask in order}
    return [got[mask] for mask in range(1, count)]


def feat_halves(partial):
    count = lax.axis_size("feat")
    mask = 1
    while mask * 2 < count:
        partial = partial + swap(partial, "feat", mask)
        mask *= 2
    return partial, swap(partial, "feat", mask)


def per_device(x_blocks, block_cols, labels, group_ids, picks, w_init):
    row_blocks, per_row, block_size, _ = x_blocks.shape
    feat_rows, classes = w_init.shape
    col_blocks = feat_rows // block_size
    total_blocks = block_cols.shape[0]
    n_samp = lax.axis_size("samp")
    n_feat = lax.axis_size("feat")
    rate = weight_rate * picks.shape[1] / (per_row * n_feat)
    sel = picks.shape[1] // n_samp
    slots = min(row_blocks, sel - 1 + LEND)
    size = col_blocks // n_samp
    direct = 2 < n_samp <= 8
    me = lax.axis_index("samp").astype(jnp.int32).reshape(1)
    label_rows = labels.reshape(total_blocks, block_size)
    gid_rows = group_ids.reshape(total_blocks, block_size)
    cols = block_cols.T
    ends = [classes * cut // 64 for cut in CUTS]
    bounds = list(zip([0] + ends[:-1], ends, strict=True))
    widths = [high - low for low, high in bounds]
    chunks = len(bounds)
    work = 2 * slots * per_row * block_size * block_size

    def blocks(count, width, dtype):
        return shape((count, width, block_size), dtype)

    slot_table, live, counts, x_data, *rest = pl.pallas_call(
        functools.partial(setup_kernel, sel, row_blocks, bounds),
        out_shape=(
            shape((STEPS, slots), jnp.int32),
            shape((STEPS, slots), jnp.int32),
            shape((STEPS, GRP, LANES), F32),
            shape(x_blocks.shape, BF16),
            *[blocks(size, width, F32) for width in widths],
            *[blocks(slots, width, F32) for width in widths],
        ),
        in_specs=[SM] + [HBM] * 5,
        out_specs=(SM, SM) + (VM,) * (2 + 2 * chunks),
        scratch_shapes=[
            pltpu.VMEM((col_blocks, classes, block_size), BF16),
            pltpu.SMEM(picks.shape, jnp.int32),
            pltpu.SMEM(cols.shape, jnp.int32),
            pltpu.VMEM(gid_rows.shape, jnp.int32),
            pltpu.VMEM((classes, feat_rows), F32),
            pltpu.SemaphoreType.DMA((4 + row_blocks,)),
        ],
        compiler_params=PARAMS,
        name="setup",
    )(me, *[pltpu.with_memory_space_constraint(each, pltpu.HBM) for each in (picks, cols, gid_rows, w_init.T, x_blocks)])
    states, partials = rest[:chunks], rest[chunks:]

    def flip(after):
        data, _ = lax.optimization_barrier((x_data, after))
        return pl.pallas_call(
            flip_kernel,
            out_shape=shape(x_blocks.shape, BF16),
            in_specs=[VM],
            out_specs=VM,
            compiler_params=PARAMS,
            cost_estimate=cost(0, 4 * x_blocks.size),
            name="flip",
        )(data)

    def forward(parts, step, width):
        count = row_blocks if step is None else slots
        return pl.pallas_call(
            functools.partial(forward_kernel, step, row_blocks),
            out_shape=blocks(count, width, F32),
            in_specs=[SM, SM, SM] + [VM] * (1 + len(parts)),
            out_specs=VM,
            scratch_shapes=[pltpu.VMEM((col_blocks, width, block_size), BF16)],
            compiler_params=PARAMS,
            cost_estimate=cost(work * width, work),
            name="forward",
        )(me, slot_table, cols, flipped[0], *parts)

    def send_shapes(rows, dtype):
        if direct:
            return (shape((rows, LANES), dtype),) * (n_samp - 1)
        return (shape((n_samp, rows, LANES), dtype),)

    def exchange(sends):
        if direct:
            return swaps(sends, "samp")
        return [lax.all_to_all(sends[0], "samp", 0, 0)]

    def collect(new_bf):
        if direct:
            return [new_bf] + swaps([new_bf] * (n_samp - 1), "samp")
        return [lax.all_gather(new_bf, "samp", axis=0, tiled=True)]

    def evaluate(halves, bases, adversary, step_q, step, keep, sent):
        sends = send_shapes(size * widths[0] + (2 * GRP if sent == BF16 else GRP), sent)
        own, loss, *rest = pl.pallas_call(
            functools.partial(grad_kernel, step, n_samp, row_blocks, bounds),
            out_shape=(
                blocks(size, widths[0], F32),
                shape((GRP, LANES), F32),
                *[blocks(slots, width, BF16) for width in widths[1:]],
                *sends,
            ),
            in_specs=[SM, SM, SM, SM] + [VM] * (5 + 2 * chunks),
            out_specs=(VM,) * (1 + chunks + len(sends)),
            scratch_shapes=[pltpu.VMEM((col_blocks, widths[0], block_size), F32)],
            compiler_params=PARAMS,
            cost_estimate=cost(work * widths[0], work),
            name="grad",
        )(me, slot_table, live, cols, x_data, label_rows, gid_rows, adversary, counts, *sum(halves, ()))
        if not flipped:
            flipped.append(flip(loss))
        rests, sends = rest[: chunks - 1], rest[chunks - 1 :]
        recvs = [exchange(sends)]
        owns = [own]
        for width, dz in zip(widths[1:], rests, strict=True):
            sends = send_shapes(size * width, sent)
            own, *sends = pl.pallas_call(
                functools.partial(more_grad_kernel, step, n_samp, row_blocks),
                out_shape=(blocks(size, width, F32), *sends),
                in_specs=[SM, SM, SM, VM, VM],
                out_specs=(VM,) * (1 + len(sends)),
                scratch_shapes=[pltpu.VMEM((col_blocks, width, block_size), F32)],
                compiler_params=PARAMS,
                cost_estimate=cost(work * width, work),
                name="more_grad",
            )(me, slot_table, cols, x_data, dz)
            owns.append(own)
            recvs.append(exchange(sends))
        news, logits = [], []
        for h, width in enumerate(widths):
            outs = (blocks(size, width, BF16),) + ((blocks(size, width, F32),) if keep else ())
            count = len(recvs[h])
            if h == 0:
                new_q, new_bf, *new = pl.pallas_call(
                    functools.partial(update_kernel, step, rate, keep, count),
                    out_shape=(shape((GRP, LANES), F32), *outs),
                    in_specs=[SM] + [VM] * (5 + count),
                    out_specs=(VM,) * (1 + len(outs)),
                    compiler_params=PARAMS,
                    name="update",
                )(me, owns[h], bases[h], loss, step_q, counts, *recvs[h][::-1])
            else:
                new_bf, *new = pl.pallas_call(
                    functools.partial(more_update_kernel, rate, keep, count),
                    out_shape=outs,
                    in_specs=[SM] + [VM] * (2 + count),
                    out_specs=(VM,) * len(outs),
                    compiler_params=PARAMS,
                    name="more_update",
                )(me, owns[h], bases[h], *recvs[h][::-1])
            news += new
            logits.append(collect(new_bf))
        return news, logits, new_q

    def halves_of(parts, step):
        return [feat_halves(forward(part, step, width)) for part, width in zip(parts, widths, strict=True)]

    flipped = []
    adversary = jnp.full((GRP, LANES), 1.0 / GRP, F32)
    halves = [feat_halves(partial) for partial in partials]
    for step in range(STEPS):
        _, parts, half_q = evaluate(halves, states, adversary, adversary, step, False, BF16 if step else F32)
        halves = halves_of(parts, step)
        states_new, parts, adversary = evaluate(halves, states, half_q, adversary, step, step + 1 < STEPS, BF16)
        if step + 1 < STEPS:
            states = states_new
            halves = halves_of(parts, step + 1)
    final = halves_of(parts, None)
    scores = pl.pallas_call(
        functools.partial(scores_kernel, bounds),
        out_shape=shape((classes, row_blocks * block_size), F32),
        in_specs=[VM] * (2 * chunks),
        out_specs=VM,
        compiler_params=PARAMS,
        name="scores",
    )(*sum(final, ()))
    return (scores.T, adversary[:, 0])


def solution(mesh):
    in_specs = (
        P(("groups", "samp"), "feat", None, None),
        P("groups", "feat"),
        P("groups"),
        P("groups"),
        P(None, "groups"),
        P("feat", None),
    )
    out_specs = (P(("groups", "samp"), None), P("groups"))
    return jax.shard_map(
        per_device, mesh=mesh, in_specs=in_specs, out_specs=out_specs, check_vma=False
    )
```

```python
import functools

import jax
import jax.numpy as jnp
from jax import lax
from jax.experimental import pallas as pl
from jax.experimental.pallas import tpu as pltpu
from jax.sharding import PartitionSpec as P

GRP = 8
STEPS = 3
LEND = 2
LANES = 128
CUTS = (64,)

weight_rate = 8.0
adv_rate = 2.0

F32 = jnp.float32
BF16 = jnp.bfloat16
VM = pl.BlockSpec(memory_space=pltpu.VMEM)
SM = pl.BlockSpec(memory_space=pltpu.SMEM)
HBM = pl.BlockSpec(memory_space=pltpu.HBM)
PARAMS = pltpu.CompilerParams(vmem_limit_bytes=24 << 20)


def shape(dims, dtype):
    return jax.ShapeDtypeStruct(dims, dtype)


def cost(flops, bytes_accessed):
    return pl.CostEstimate(flops=flops, bytes_accessed=bytes_accessed, transcendentals=0)


def lane_sum(rows):
    return jnp.broadcast_to(jnp.sum(rows, axis=1, keepdims=True), rows.shape)


def tree_sum(parts):
    while len(parts) > 1:
        parts = [a + b for a, b in zip(parts[::2], parts[1::2], strict=True)]
    return parts[0]


def group_hot(row):
    return (lax.broadcasted_iota(jnp.int32, (GRP, LANES), 0) == row).astype(F32)


def row_data(x_ref, row):
    return jnp.concatenate([x_ref[row, j] for j in range(x_ref.shape[1])], axis=1)


def setup_kernel(
    sel, row_blocks, bounds, me_ref, picks_hbm, cols_hbm, gid_hbm, w_hbm, x_hbm, slots_ref, live_ref, counts_ref, xv_ref,
    *refs
):
    chunks = len(bounds)
    owns, zs = refs[:chunks], refs[chunks : 2 * chunks]
    wall, picks_ref, cols_ref, gid_ref, w_ref, sems = refs[2 * chunks :]

    def fetch(source, target, place):
        copy = pltpu.make_async_copy(source, target, sems.at[place])
        copy.start()
        return copy

    get_picks = fetch(picks_hbm, picks_ref, 0)
    get_w = fetch(w_hbm, w_ref, 1)
    get_cols = fetch(cols_hbm, cols_ref, 2)
    get_gid = fetch(gid_hbm, gid_ref, 3)
    get_rows = [fetch(x_hbm.at[row], xv_ref.at[row], 4 + row) for row in range(row_blocks)]
    slots = slots_ref.shape[1]
    me = (me_ref[0] >> 1)
    samp_count = picks_ref.shape[1] // sel
    before = lax.rem(me + samp_count - 1, samp_count)
    for step in range(STEPS):
        for slot in range(slots):
            slots_ref[step, slot] = 0
            live_ref[step, slot] = 0
    get_picks.wait()
    for step in range(STEPS):
        found = jnp.int32(0)
        for start in (me * sel, before * sel):
            for entry in range(sel):
                block = picks_ref[step, start + entry]
                mine = (block // row_blocks) == me
                place = jnp.minimum(found, slots - 1)

                @pl.when(mine)
                def _(step=step, place=place, block=block):
                    slots_ref[step, place] = block - me * row_blocks
                    live_ref[step, place] = 1

                found = found + mine.astype(jnp.int32)
    get_w.wait()
    for col in range(wall.shape[0]):
        wall[col] = w_ref[:, col * LANES : (col + 1) * LANES].astype(BF16)
    size = owns[0].shape[0]
    for col in range(size):
        start = pl.multiple_of((me * size + col) * LANES, LANES)
        for own, (low, high) in zip(owns, bounds, strict=True):
            own[col] = w_ref[low:high, pl.ds(start, LANES)]
    get_gid.wait()
    for step in range(STEPS):

        def count(entry, total, step=step):
            return total + group_hot(gid_ref[pl.ds(picks_ref[step, entry], 1), :])

        total = lax.fori_loop(0, picks_ref.shape[1], count, jnp.zeros((GRP, LANES), F32))
        counts_ref[step] = lane_sum(total)
    get_cols.wait()
    for copy in get_rows:
        copy.wait()
    for slot in range(slots):
        row = slots_ref[0, slot]
        tiles = jnp.concatenate([wall[cols_ref[j, me * row_blocks + row]] for j in range(xv_ref.shape[1])], axis=1)
        piece = lax.dot_general(
            tiles, row_data(xv_ref, row), (((1,), (1,)), ((), ())), preferred_element_type=F32
        )
        for z, (low, high) in zip(zs, bounds, strict=True):
            z[slot] = piece[low:high]


def flip_kernel(x_ref, out_ref):
    for row in range(x_ref.shape[0]):
        for j in range(x_ref.shape[1]):
            out_ref[row, j] = x_ref[row, j].T


def join_classes(core, own, other):
    return jnp.concatenate([jnp.where(core == 0, own, other), jnp.where(core == 0, other, own)], axis=0)


def forward_kernel(step, row_blocks, me_ref, slots_ref, cols_ref, xt_ref, *refs):
    count = 2 if step is None else 1
    parts, outs, wall = refs[: -1 - count], refs[-1 - count : -1], refs[-1]
    me = (me_ref[0] >> 1)
    per_row, depth, rows = xt_ref.shape[1:]
    if len(parts) > 1:
        size = parts[0].shape[0]
        for mask in range(len(parts)):
            start = (me ^ mask) * size
            for col in range(size):
                wall[start + col] = parts[mask][col]
        weights = wall
    else:
        weights = parts[0]
    for slot in range(outs[0].shape[0]):
        row = slot if step is None else slots_ref[step, slot]
        tiles = jnp.concatenate([weights[cols_ref[j, me * row_blocks + row]] for j in range(per_row)], axis=1)
        piece = jnp.dot(tiles, xt_ref[row].reshape(per_row * depth, rows), preferred_element_type=F32)
        if step is None:
            half = outs[0].shape[1]
            outs[0][slot] = jnp.where((me_ref[0] & 1) == 0, piece[:half], piece[half:])
            outs[1][slot] = jnp.where((me_ref[0] & 1) == 0, piece[half:], piece[:half])
        else:
            outs[0][slot] = piece


def send_out(n_samp, me, acc, own_ref, sends, tail):
    size, classes, _ = own_ref.shape
    rows = size * classes
    for col in range(size):
        own_ref[col] = acc[me * size + col]
    if len(sends) == 1:
        for owner in range(n_samp):
            for col in range(size):
                sends[0][owner, col * classes : (col + 1) * classes, :] = acc[owner * size + col].astype(
                    sends[0].dtype
                )
            if tail is not None:
                sends[0][owner, rows : rows + tail.shape[0], :] = tail
        return
    for mask in range(1, n_samp):
        send = sends[mask - 1]
        start = (me ^ mask) * size
        for col in range(size):
            send[col * classes : (col + 1) * classes, :] = acc[start + col].astype(send.dtype)
        if tail is not None:
            send[rows : rows + tail.shape[0], :] = tail


def add_pieces(acc, cols_ref, row, piece):
    for j in range(cols_ref.shape[0]):
        col = cols_ref[j, row]
        acc[col] = acc[col] + piece[:, j * LANES : (j + 1) * LANES]


def grad_kernel(
    step, n_samp, row_blocks, bounds, me_ref, slots_ref, live_ref, cols_ref, x_ref, label_ref, gid_ref, q_ref, counts_ref,
    *refs
):
    chunks = len(bounds)
    halves, refs = refs[: 2 * chunks], refs[2 * chunks :]
    (own_ref, loss_ref), rests, refs = refs[:2], refs[2 : 1 + chunks], refs[1 + chunks :]
    sends, acc = refs[:-1], refs[-1]
    me = (me_ref[0] >> 1)
    acc[...] = jnp.zeros_like(acc)
    classes = bounds[-1][1]
    weight = q_ref[...] / counts_ref[step]
    loss = jnp.zeros((GRP, LANES), F32)
    for slot in range(slots_ref.shape[1]):
        local = slots_ref[step, slot]
        row = me * row_blocks + local
        mult = live_ref[step, slot].astype(F32)
        logits = jnp.concatenate([halves[2 * h][slot] + halves[2 * h + 1][slot] for h in range(chunks)], axis=0)
        hot = (
            lax.broadcasted_iota(jnp.int32, (classes, LANES), 0) == label_ref[pl.ds(row, 1), :]
        ).astype(F32)
        groups = group_hot(gid_ref[pl.ds(row, 1), :])
        top = jnp.max(logits, axis=0, keepdims=True)
        log_total = top + jnp.log(jnp.sum(jnp.exp(logits - top), axis=0, keepdims=True))
        cross = log_total - jnp.sum(logits * hot, axis=0, keepdims=True)
        probs = jnp.exp(logits - log_total)
        loss = loss + groups * (mult * cross)
        coef = jnp.sum(groups * weight, axis=0, keepdims=True) * mult
        dz = (coef * (probs - hot)).astype(BF16)
        for rest, (low, high) in zip(rests, bounds[1:], strict=True):
            rest[slot] = dz[low:high]
        piece = jnp.dot(dz[: bounds[0][1]], row_data(x_ref, local), preferred_element_type=F32)
        add_pieces(acc, cols_ref, row, piece)
    loss = lane_sum(loss)
    loss_ref[...] = loss
    tail = loss
    if sends[0].dtype == BF16:
        high = loss.astype(BF16).astype(F32)
        rest = loss - high
        middle = rest.astype(BF16).astype(F32)
        low = rest - middle
        left = lax.broadcasted_iota(jnp.int32, (GRP, LANES), 1) < LANES // 2
        tail = jnp.concatenate([jnp.where(left, high, low), middle], axis=0).astype(BF16)
    send_out(n_samp, me, acc, own_ref, sends, tail)


def more_grad_kernel(step, n_samp, row_blocks, me_ref, slots_ref, cols_ref, x_ref, dz_ref, own_ref, *refs):
    sends, acc = refs[:-1], refs[-1]
    me = (me_ref[0] >> 1)
    acc[...] = jnp.zeros_like(acc)
    for slot in range(slots_ref.shape[1]):
        local = slots_ref[step, slot]
        piece = jnp.dot(dz_ref[slot], row_data(x_ref, local), preferred_element_type=F32)
        add_pieces(acc, cols_ref, me * row_blocks + local, piece)
    send_out(n_samp, me, acc, own_ref, sends, None)


def new_weights(rate, me_ref, own_ref, w_ref, recvs, w_out, wbf_out):
    size, classes, _ = own_ref.shape
    for col in range(size):
        span = slice(col * classes, (col + 1) * classes)
        own = own_ref[col]
        if len(recvs) == 1:
            parts = [
                jnp.where((me_ref[0] >> 1) == i, own, recvs[0][i, span, :].astype(F32)) for i in range(recvs[0].shape[0])
            ]
        else:
            parts = [own] + [recv[span, :].astype(F32) for recv in recvs]
        state = w_ref[col] - rate * tree_sum(parts)
        if w_out is not None:
            w_out[col] = state
        wbf_out[col] = state.astype(BF16)


def update_kernel(step, rate, keep, count, me_ref, own_ref, w_ref, loss_ref, q_ref, counts_ref, *refs):
    recvs, outs = list(refs[:count])[::-1], list(refs[count:])
    size, classes, _ = own_ref.shape
    rows = size * classes
    more = 2 * GRP if recvs[0].dtype == BF16 else GRP

    def loss_of(tail):
        if tail.dtype == F32:
            return tail[:, :1]
        tail = tail.astype(F32)
        return (tail[:GRP, :1] + tail[GRP:, :1]) + tail[:GRP, LANES // 2 : LANES // 2 + 1]

    if len(recvs) == 1:
        loss = tree_sum([loss_of(recvs[0][i, rows : rows + more, :]) for i in range(recvs[0].shape[0])])
    else:
        loss = tree_sum([loss_ref[:, :1]] + [loss_of(recv[rows : rows + more, :]) for recv in recvs])
    score = jnp.log(q_ref[...]) + adv_rate * (loss / counts_ref[step])
    grown = jnp.exp(score - jnp.max(score, axis=0, keepdims=True))
    outs[0][...] = grown / jnp.sum(grown, axis=0, keepdims=True)
    new_weights(rate, me_ref, own_ref, w_ref, recvs, outs[2] if keep else None, outs[1])


def more_update_kernel(rate, keep, count, me_ref, own_ref, w_ref, *refs):
    recvs, outs = list(refs[:count])[::-1], list(refs[count:])
    new_weights(rate, me_ref, own_ref, w_ref, recvs, outs[1] if keep else None, outs[0])


def scores_kernel(me_ref, mine_ref, other_ref, out_ref):
    for block in range(mine_ref.shape[0]):
        out_ref[:, block * LANES : (block + 1) * LANES] = join_classes((me_ref[0] & 1), mine_ref[block], other_ref[block])


def swap(value, axis, mask):
    count = lax.axis_size(axis)
    return lax.ppermute(value, axis, [(i, i ^ mask) for i in range(count)])


def swaps(values, axis):
    count = len(values) + 1
    order = sorted(range(1, count), key=lambda mask: (mask < count // 2, mask))
    got = {mask: swap(values[mask - 1], axis, mask) for mask in order}
    return [got[mask] for mask in range(1, count)]


def feat_halves(partial):
    count = lax.axis_size("feat")
    mask = 1
    while mask * 2 < count:
        partial = partial + swap(partial, "feat", mask)
        mask *= 2
    return partial, swap(partial, "feat", mask)


def per_device(x_blocks, block_cols, labels, group_ids, picks, w_init):
    row_blocks, per_row, block_size, _ = x_blocks.shape
    feat_rows, classes = w_init.shape
    col_blocks = feat_rows // block_size
    total_blocks = block_cols.shape[0]
    n_samp = lax.axis_size("samp")
    n_feat = lax.axis_size("feat")
    rate = weight_rate * picks.shape[1] / (per_row * n_feat)
    sel = picks.shape[1] // n_samp
    slots = min(row_blocks, sel - 1 + LEND)
    size = col_blocks // n_samp
    direct = 2 < n_samp <= 8
    me = (lax.axis_index("samp") * 2 + (lax.axis_index("feat") & 1)).astype(jnp.int32).reshape(1)
    label_rows = labels.reshape(total_blocks, block_size)
    gid_rows = group_ids.reshape(total_blocks, block_size)
    cols = block_cols.T
    ends = [classes * cut // 64 for cut in CUTS]
    bounds = list(zip([0] + ends[:-1], ends, strict=True))
    widths = [high - low for low, high in bounds]
    chunks = len(bounds)
    work = 2 * slots * per_row * block_size * block_size

    def blocks(count, width, dtype):
        return shape((count, width, block_size), dtype)

    slot_table, live, counts, x_data, *rest = pl.pallas_call(
        functools.partial(setup_kernel, sel, row_blocks, bounds),
        out_shape=(
            shape((STEPS, slots), jnp.int32),
            shape((STEPS, slots), jnp.int32),
            shape((STEPS, GRP, LANES), F32),
            shape(x_blocks.shape, BF16),
            *[blocks(size, width, F32) for width in widths],
            *[blocks(slots, width, F32) for width in widths],
        ),
        in_specs=[SM] + [HBM] * 5,
        out_specs=(SM, SM) + (VM,) * (2 + 2 * chunks),
        scratch_shapes=[
            pltpu.VMEM((col_blocks, classes, block_size), BF16),
            pltpu.SMEM(picks.shape, jnp.int32),
            pltpu.SMEM(cols.shape, jnp.int32),
            pltpu.VMEM(gid_rows.shape, jnp.int32),
            pltpu.VMEM((classes, feat_rows), F32),
            pltpu.SemaphoreType.DMA((4 + row_blocks,)),
        ],
        compiler_params=PARAMS,
        name="setup",
    )(me, *[pltpu.with_memory_space_constraint(each, pltpu.HBM) for each in (picks, cols, gid_rows, w_init.T, x_blocks)])
    states, partials = rest[:chunks], rest[chunks:]

    def flip(after):
        data, _ = lax.optimization_barrier((x_data, after))
        return pl.pallas_call(
            flip_kernel,
            out_shape=shape(x_blocks.shape, BF16),
            in_specs=[VM],
            out_specs=VM,
            compiler_params=PARAMS,
            cost_estimate=cost(0, 4 * x_blocks.size),
            name="flip",
        )(data)

    def forward(parts, step, width):
        if step is None:
            outs = (blocks(row_blocks, width // 2, F32),) * 2
        else:
            outs = (blocks(slots, width, F32),)
        return pl.pallas_call(
            functools.partial(forward_kernel, step, row_blocks),
            out_shape=outs,
            in_specs=[SM, SM, SM] + [VM] * (1 + len(parts)),
            out_specs=(VM,) * len(outs),
            scratch_shapes=[pltpu.VMEM((col_blocks, width, block_size), BF16)],
            compiler_params=PARAMS,
            cost_estimate=cost(work * width, work),
            name="forward",
        )(me, slot_table, cols, flipped[0], *parts)

    def send_shapes(rows, dtype):
        if direct:
            return (shape((rows, LANES), dtype),) * (n_samp - 1)
        return (shape((n_samp, rows, LANES), dtype),)

    def exchange(sends):
        if direct:
            return swaps(sends, "samp")
        return [lax.all_to_all(sends[0], "samp", 0, 0)]

    def collect(new_bf):
        if direct:
            return [new_bf] + swaps([new_bf] * (n_samp - 1), "samp")
        return [lax.all_gather(new_bf, "samp", axis=0, tiled=True)]

    def evaluate(halves, bases, adversary, step_q, step, keep, sent):
        sends = send_shapes(size * widths[0] + (2 * GRP if sent == BF16 else GRP), sent)
        own, loss, *rest = pl.pallas_call(
            functools.partial(grad_kernel, step, n_samp, row_blocks, bounds),
            out_shape=(
                blocks(size, widths[0], F32),
                shape((GRP, LANES), F32),
                *[blocks(slots, width, BF16) for width in widths[1:]],
                *sends,
            ),
            in_specs=[SM, SM, SM, SM] + [VM] * (5 + 2 * chunks),
            out_specs=(VM,) * (1 + chunks + len(sends)),
            scratch_shapes=[pltpu.VMEM((col_blocks, widths[0], block_size), F32)],
            compiler_params=PARAMS,
            cost_estimate=cost(work * widths[0], work),
            name="grad",
        )(me, slot_table, live, cols, x_data, label_rows, gid_rows, adversary, counts, *sum(halves, ()))
        if not flipped:
            flipped.append(flip(loss))
        rests, sends = rest[: chunks - 1], rest[chunks - 1 :]
        recvs = [exchange(sends)]
        owns = [own]
        for width, dz in zip(widths[1:], rests, strict=True):
            sends = send_shapes(size * width, sent)
            own, *sends = pl.pallas_call(
                functools.partial(more_grad_kernel, step, n_samp, row_blocks),
                out_shape=(blocks(size, width, F32), *sends),
                in_specs=[SM, SM, SM, VM, VM],
                out_specs=(VM,) * (1 + len(sends)),
                scratch_shapes=[pltpu.VMEM((col_blocks, width, block_size), F32)],
                compiler_params=PARAMS,
                cost_estimate=cost(work * width, work),
                name="more_grad",
            )(me, slot_table, cols, x_data, dz)
            owns.append(own)
            recvs.append(exchange(sends))
        news, logits = [], []
        for h, width in enumerate(widths):
            outs = (blocks(size, width, BF16),) + ((blocks(size, width, F32),) if keep else ())
            count = len(recvs[h])
            if h == 0:
                new_q, new_bf, *new = pl.pallas_call(
                    functools.partial(update_kernel, step, rate, keep, count),
                    out_shape=(shape((GRP, LANES), F32), *outs),
                    in_specs=[SM] + [VM] * (5 + count),
                    out_specs=(VM,) * (1 + len(outs)),
                    compiler_params=PARAMS,
                    name="update",
                )(me, owns[h], bases[h], loss, step_q, counts, *recvs[h][::-1])
            else:
                new_bf, *new = pl.pallas_call(
                    functools.partial(more_update_kernel, rate, keep, count),
                    out_shape=outs,
                    in_specs=[SM] + [VM] * (2 + count),
                    out_specs=(VM,) * len(outs),
                    compiler_params=PARAMS,
                    name="more_update",
                )(me, owns[h], bases[h], *recvs[h][::-1])
            news += new
            logits.append(collect(new_bf))
        return news, logits, new_q

    def halves_of(parts, step):
        return [feat_halves(forward(part, step, width)[0]) for part, width in zip(parts, widths, strict=True)]

    flipped = []
    adversary = jnp.full((GRP, LANES), 1.0 / GRP, F32)
    halves = [feat_halves(partial) for partial in partials]
    for step in range(STEPS):
        _, parts, half_q = evaluate(halves, states, adversary, adversary, step, False, BF16 if step else F32)
        halves = halves_of(parts, step)
        states_new, parts, adversary = evaluate(halves, states, half_q, adversary, step, step + 1 < STEPS, BF16)
        if step + 1 < STEPS:
            states = states_new
            halves = halves_of(parts, step + 1)
    mine, give = forward(parts[0], None, classes)
    mine, mask = mine + swap(give, "feat", 1), 2
    while mask < n_feat:
        mine = mine + swap(mine, "feat", mask)
        mask *= 2
    scores = pl.pallas_call(
        scores_kernel,
        out_shape=shape((classes, row_blocks * block_size), F32),
        in_specs=[SM, VM, VM],
        out_specs=VM,
        compiler_params=PARAMS,
        name="scores",
    )(me, mine, swap(mine, "feat", 1))
    return (scores.T, adversary[:, 0])


def solution(mesh):
    in_specs = (
        P(("groups", "samp"), "feat", None, None),
        P("groups", "feat"),
        P("groups"),
        P("groups"),
        P(None, "groups"),
        P("feat", None),
    )
    out_specs = (P(("groups", "samp"), None), P("groups"))
    return jax.shard_map(
        per_device, mesh=mesh, in_specs=in_specs, out_specs=out_specs, check_vma=False
    )
```

```python
import functools

import jax
import jax.numpy as jnp
from jax import lax
from jax.experimental import pallas as pl
from jax.experimental.pallas import tpu as pltpu
from jax.sharding import PartitionSpec as P

GRP = 8
STEPS = 3
LEND = 2
LANES = 128
CUTS = (64,)

weight_rate = 8.0
adv_rate = 2.0

F32 = jnp.float32
BF16 = jnp.bfloat16
VM = pl.BlockSpec(memory_space=pltpu.VMEM)
SM = pl.BlockSpec(memory_space=pltpu.SMEM)
HBM = pl.BlockSpec(memory_space=pltpu.HBM)
PARAMS = pltpu.CompilerParams(vmem_limit_bytes=24 << 20)


def shape(dims, dtype):
    return jax.ShapeDtypeStruct(dims, dtype)


def cost(flops, bytes_accessed):
    return pl.CostEstimate(flops=flops, bytes_accessed=bytes_accessed, transcendentals=0)


def lane_sum(rows):
    return jnp.broadcast_to(jnp.sum(rows, axis=1, keepdims=True), rows.shape)


def tree_sum(parts):
    while len(parts) > 1:
        parts = [a + b for a, b in zip(parts[::2], parts[1::2], strict=True)]
    return parts[0]


def group_hot(row):
    return (lax.broadcasted_iota(jnp.int32, (GRP, LANES), 0) == row).astype(F32)


def row_data(x_ref, row):
    return jnp.concatenate([x_ref[row, j] for j in range(x_ref.shape[1])], axis=1)


def setup_kernel(
    sel, row_blocks, bounds, me_ref, picks_hbm, cols_hbm, gid_hbm, w_hbm, x_hbm, slots_ref, live_ref, counts_ref, xv_ref,
    *refs
):
    chunks = len(bounds)
    owns, zs = refs[:chunks], refs[chunks : 2 * chunks]
    wall, picks_ref, cols_ref, slot_of, gid_ref, w_ref, sems = refs[2 * chunks :]

    def fetch(source, target, place):
        copy = pltpu.make_async_copy(source, target, sems.at[place])
        copy.start()
        return copy

    get_picks = fetch(picks_hbm, picks_ref, 0)
    get_w = fetch(w_hbm, w_ref, 1)
    get_cols = fetch(cols_hbm, cols_ref, 2)
    get_gid = fetch(gid_hbm, gid_ref, 3)
    get_rows = [fetch(x_hbm.at[row], xv_ref.at[row], 4 + row) for row in range(row_blocks)]
    slots = slots_ref.shape[1]
    me = (me_ref[0] >> 1)
    samp_count = picks_ref.shape[1] // sel
    before = lax.rem(me + samp_count - 1, samp_count)
    for step in range(STEPS):
        for slot in range(slots):
            slots_ref[step, slot] = 0
            live_ref[step, slot] = 0
    for row in range(row_blocks):
        slot_of[row] = -1
    for z in zs:
        z[...] = jnp.zeros_like(z)
    get_picks.wait()
    for step in range(STEPS):
        found = jnp.int32(0)
        for start in (me * sel, before * sel):
            for entry in range(sel):
                block = picks_ref[step, start + entry]
                mine = (block // row_blocks) == me
                place = jnp.minimum(found, slots - 1)

                @pl.when(mine)
                def _(step=step, place=place, block=block):
                    slots_ref[step, place] = block - me * row_blocks
                    live_ref[step, place] = 1
                    if step == 0:
                        slot_of[block - me * row_blocks] = place

                found = found + mine.astype(jnp.int32)
    get_w.wait()
    for col in range(wall.shape[0]):
        wall[col] = w_ref[:, col * LANES : (col + 1) * LANES].astype(BF16)
    size = owns[0].shape[0]
    for col in range(size):
        start = pl.multiple_of((me * size + col) * LANES, LANES)
        for own, (low, high) in zip(owns, bounds, strict=True):
            own[col] = w_ref[low:high, pl.ds(start, LANES)]
    get_gid.wait()
    for step in range(STEPS):

        def count(entry, total, step=step):
            return total + group_hot(gid_ref[pl.ds(picks_ref[step, entry], 1), :])

        total = lax.fori_loop(0, picks_ref.shape[1], count, jnp.zeros((GRP, LANES), F32))
        counts_ref[step] = lane_sum(total)
    get_cols.wait()
    for row, copy in enumerate(get_rows):
        copy.wait()

        @pl.when(slot_of[row] >= 0)
        def _(row=row):
            tiles = jnp.concatenate([wall[cols_ref[j, me * row_blocks + row]] for j in range(xv_ref.shape[1])], axis=1)
            piece = lax.dot_general(
                tiles, row_data(xv_ref, row), (((1,), (1,)), ((), ())), preferred_element_type=F32
            )
            for z, (low, high) in zip(zs, bounds, strict=True):
                z[slot_of[row]] = piece[low:high]


def flip_kernel(x_ref, out_ref):
    for row in range(x_ref.shape[0]):
        for j in range(x_ref.shape[1]):
            out_ref[row, j] = x_ref[row, j].T


def join_classes(core, own, other):
    return jnp.concatenate([jnp.where(core == 0, own, other), jnp.where(core == 0, other, own)], axis=0)


def forward_kernel(step, row_blocks, me_ref, slots_ref, cols_ref, xt_ref, *refs):
    count = 2 if step is None else 1
    parts, outs, wall = refs[: -1 - count], refs[-1 - count : -1], refs[-1]
    me = (me_ref[0] >> 1)
    per_row, depth, rows = xt_ref.shape[1:]
    if len(parts) > 1:
        size = parts[0].shape[0]
        for mask in range(len(parts)):
            start = (me ^ mask) * size
            for col in range(size):
                wall[start + col] = parts[mask][col]
        weights = wall
    else:
        weights = parts[0]
    for slot in range(outs[0].shape[0]):
        row = slot if step is None else slots_ref[step, slot]
        tiles = jnp.concatenate([weights[cols_ref[j, me * row_blocks + row]] for j in range(per_row)], axis=1)
        piece = jnp.dot(tiles, xt_ref[row].reshape(per_row * depth, rows), preferred_element_type=F32)
        if step is None:
            half = outs[0].shape[1]
            outs[0][slot] = jnp.where((me_ref[0] & 1) == 0, piece[:half], piece[half:])
            outs[1][slot] = jnp.where((me_ref[0] & 1) == 0, piece[half:], piece[:half])
        else:
            outs[0][slot] = piece


def send_out(n_samp, me, acc, own_ref, sends, tail):
    size, classes, _ = own_ref.shape
    rows = size * classes
    for col in range(size):
        own_ref[col] = acc[me * size + col]
    if len(sends) == 1:
        for owner in range(n_samp):
            for col in range(size):
                sends[0][owner, col * classes : (col + 1) * classes, :] = acc[owner * size + col].astype(
                    sends[0].dtype
                )
            if tail is not None:
                sends[0][owner, rows : rows + tail.shape[0], :] = tail
        return
    for mask in range(1, n_samp):
        send = sends[mask - 1]
        start = (me ^ mask) * size
        for col in range(size):
            send[col * classes : (col + 1) * classes, :] = acc[start + col].astype(send.dtype)
        if tail is not None:
            send[rows : rows + tail.shape[0], :] = tail


def add_pieces(acc, cols_ref, row, piece):
    for j in range(cols_ref.shape[0]):
        col = cols_ref[j, row]
        acc[col] = acc[col] + piece[:, j * LANES : (j + 1) * LANES]


def grad_kernel(
    step, n_samp, row_blocks, bounds, me_ref, slots_ref, live_ref, cols_ref, x_ref, label_ref, gid_ref, q_ref, counts_ref,
    *refs
):
    chunks = len(bounds)
    halves, refs = refs[: 2 * chunks], refs[2 * chunks :]
    (own_ref, loss_ref), rests, refs = refs[:2], refs[2 : 1 + chunks], refs[1 + chunks :]
    sends, acc = refs[:-1], refs[-1]
    me = (me_ref[0] >> 1)
    acc[...] = jnp.zeros_like(acc)
    classes = bounds[-1][1]
    weight = q_ref[...] / counts_ref[step]
    loss = jnp.zeros((GRP, LANES), F32)
    for slot in range(slots_ref.shape[1]):
        local = slots_ref[step, slot]
        row = me * row_blocks + local
        mult = live_ref[step, slot].astype(F32)
        logits = jnp.concatenate([halves[2 * h][slot] + halves[2 * h + 1][slot] for h in range(chunks)], axis=0)
        hot = (
            lax.broadcasted_iota(jnp.int32, (classes, LANES), 0) == label_ref[pl.ds(row, 1), :]
        ).astype(F32)
        groups = group_hot(gid_ref[pl.ds(row, 1), :])
        top = jnp.max(logits, axis=0, keepdims=True)
        log_total = top + jnp.log(jnp.sum(jnp.exp(logits - top), axis=0, keepdims=True))
        cross = log_total - jnp.sum(logits * hot, axis=0, keepdims=True)
        probs = jnp.exp(logits - log_total)
        loss = loss + groups * (mult * cross)
        coef = jnp.sum(groups * weight, axis=0, keepdims=True) * mult
        dz = (coef * (probs - hot)).astype(BF16)
        for rest, (low, high) in zip(rests, bounds[1:], strict=True):
            rest[slot] = dz[low:high]
        piece = jnp.dot(dz[: bounds[0][1]], row_data(x_ref, local), preferred_element_type=F32)
        add_pieces(acc, cols_ref, row, piece)
    loss = lane_sum(loss)
    loss_ref[...] = loss
    tail = loss
    if sends[0].dtype == BF16:
        high = loss.astype(BF16).astype(F32)
        rest = loss - high
        middle = rest.astype(BF16).astype(F32)
        low = rest - middle
        left = lax.broadcasted_iota(jnp.int32, (GRP, LANES), 1) < LANES // 2
        tail = jnp.concatenate([jnp.where(left, high, low), middle], axis=0).astype(BF16)
    send_out(n_samp, me, acc, own_ref, sends, tail)


def more_grad_kernel(step, n_samp, row_blocks, me_ref, slots_ref, cols_ref, x_ref, dz_ref, own_ref, *refs):
    sends, acc = refs[:-1], refs[-1]
    me = (me_ref[0] >> 1)
    acc[...] = jnp.zeros_like(acc)
    for slot in range(slots_ref.shape[1]):
        local = slots_ref[step, slot]
        piece = jnp.dot(dz_ref[slot], row_data(x_ref, local), preferred_element_type=F32)
        add_pieces(acc, cols_ref, me * row_blocks + local, piece)
    send_out(n_samp, me, acc, own_ref, sends, None)


def new_weights(rate, me_ref, own_ref, w_ref, recvs, w_out, wbf_out):
    size, classes, _ = own_ref.shape
    for col in range(size):
        span = slice(col * classes, (col + 1) * classes)
        own = own_ref[col]
        if len(recvs) == 1:
            parts = [
                jnp.where((me_ref[0] >> 1) == i, own, recvs[0][i, span, :].astype(F32)) for i in range(recvs[0].shape[0])
            ]
        else:
            parts = [own] + [recv[span, :].astype(F32) for recv in recvs]
        state = w_ref[col] - rate * tree_sum(parts)
        if w_out is not None:
            w_out[col] = state
        wbf_out[col] = state.astype(BF16)


def update_kernel(step, rate, keep, count, me_ref, own_ref, w_ref, loss_ref, q_ref, counts_ref, *refs):
    recvs, outs = list(refs[:count])[::-1], list(refs[count:])
    size, classes, _ = own_ref.shape
    rows = size * classes
    more = 2 * GRP if recvs[0].dtype == BF16 else GRP

    def loss_of(tail):
        if tail.dtype == F32:
            return tail[:, :1]
        tail = tail.astype(F32)
        return (tail[:GRP, :1] + tail[GRP:, :1]) + tail[:GRP, LANES // 2 : LANES // 2 + 1]

    if len(recvs) == 1:
        loss = tree_sum([loss_of(recvs[0][i, rows : rows + more, :]) for i in range(recvs[0].shape[0])])
    else:
        loss = tree_sum([loss_ref[:, :1]] + [loss_of(recv[rows : rows + more, :]) for recv in recvs])
    score = jnp.log(q_ref[...]) + adv_rate * (loss / counts_ref[step])
    grown = jnp.exp(score - jnp.max(score, axis=0, keepdims=True))
    outs[0][...] = grown / jnp.sum(grown, axis=0, keepdims=True)
    new_weights(rate, me_ref, own_ref, w_ref, recvs, outs[2] if keep else None, outs[1])


def more_update_kernel(rate, keep, count, me_ref, own_ref, w_ref, *refs):
    recvs, outs = list(refs[:count])[::-1], list(refs[count:])
    new_weights(rate, me_ref, own_ref, w_ref, recvs, outs[1] if keep else None, outs[0])


def scores_kernel(me_ref, mine_ref, other_ref, out_ref):
    for block in range(mine_ref.shape[0]):
        out_ref[:, block * LANES : (block + 1) * LANES] = join_classes((me_ref[0] & 1), mine_ref[block], other_ref[block])


def swap(value, axis, mask):
    count = lax.axis_size(axis)
    return lax.ppermute(value, axis, [(i, i ^ mask) for i in range(count)])


def swaps(values, axis):
    count = len(values) + 1
    order = sorted(range(1, count), key=lambda mask: (mask < count // 2, mask))
    got = {mask: swap(values[mask - 1], axis, mask) for mask in order}
    return [got[mask] for mask in range(1, count)]


def feat_halves(partial):
    count = lax.axis_size("feat")
    mask = 1
    while mask * 2 < count:
        partial = partial + swap(partial, "feat", mask)
        mask *= 2
    return partial, swap(partial, "feat", mask)


def per_device(x_blocks, block_cols, labels, group_ids, picks, w_init):
    row_blocks, per_row, block_size, _ = x_blocks.shape
    feat_rows, classes = w_init.shape
    col_blocks = feat_rows // block_size
    total_blocks = block_cols.shape[0]
    n_samp = lax.axis_size("samp")
    n_feat = lax.axis_size("feat")
    rate = weight_rate * picks.shape[1] / (per_row * n_feat)
    sel = picks.shape[1] // n_samp
    slots = min(row_blocks, sel - 1 + LEND)
    size = col_blocks // n_samp
    direct = 2 < n_samp <= 8
    me = (lax.axis_index("samp") * 2 + (lax.axis_index("feat") & 1)).astype(jnp.int32).reshape(1)
    label_rows = labels.reshape(total_blocks, block_size)
    gid_rows = group_ids.reshape(total_blocks, block_size)
    cols = block_cols.T
    ends = [classes * cut // 64 for cut in CUTS]
    bounds = list(zip([0] + ends[:-1], ends, strict=True))
    widths = [high - low for low, high in bounds]
    chunks = len(bounds)
    work = 2 * slots * per_row * block_size * block_size

    def blocks(count, width, dtype):
        return shape((count, width, block_size), dtype)

    slot_table, live, counts, x_data, *rest = pl.pallas_call(
        functools.partial(setup_kernel, sel, row_blocks, bounds),
        out_shape=(
            shape((STEPS, slots), jnp.int32),
            shape((STEPS, slots), jnp.int32),
            shape((STEPS, GRP, LANES), F32),
            shape(x_blocks.shape, BF16),
            *[blocks(size, width, F32) for width in widths],
            *[blocks(slots, width, F32) for width in widths],
        ),
        in_specs=[SM] + [HBM] * 5,
        out_specs=(SM, SM) + (VM,) * (2 + 2 * chunks),
        scratch_shapes=[
            pltpu.VMEM((col_blocks, classes, block_size), BF16),
            pltpu.SMEM(picks.shape, jnp.int32),
            pltpu.SMEM(cols.shape, jnp.int32),
            pltpu.SMEM((row_blocks,), jnp.int32),
            pltpu.VMEM(gid_rows.shape, jnp.int32),
            pltpu.VMEM((classes, feat_rows), F32),
            pltpu.SemaphoreType.DMA((4 + row_blocks,)),
        ],
        compiler_params=PARAMS,
        name="setup",
    )(me, *[pltpu.with_memory_space_constraint(each, pltpu.HBM) for each in (picks, cols, gid_rows, w_init.T, x_blocks)])
    states, partials = rest[:chunks], rest[chunks:]

    def flip(after):
        data, _ = lax.optimization_barrier((x_data, after))
        return pl.pallas_call(
            flip_kernel,
            out_shape=shape(x_blocks.shape, BF16),
            in_specs=[VM],
            out_specs=VM,
            compiler_params=PARAMS,
            cost_estimate=cost(0, 4 * x_blocks.size),
            name="flip",
        )(data)

    def forward(parts, step, width):
        if step is None:
            outs = (blocks(row_blocks, width // 2, F32),) * 2
        else:
            outs = (blocks(slots, width, F32),)
        return pl.pallas_call(
            functools.partial(forward_kernel, step, row_blocks),
            out_shape=outs,
            in_specs=[SM, SM, SM] + [VM] * (1 + len(parts)),
            out_specs=(VM,) * len(outs),
            scratch_shapes=[pltpu.VMEM((col_blocks, width, block_size), BF16)],
            compiler_params=PARAMS,
            cost_estimate=cost(work * width, work),
            name="forward",
        )(me, slot_table, cols, flipped[0], *parts)

    def send_shapes(rows, dtype):
        if direct:
            return (shape((rows, LANES), dtype),) * (n_samp - 1)
        return (shape((n_samp, rows, LANES), dtype),)

    def exchange(sends):
        if direct:
            return swaps(sends, "samp")
        return [lax.all_to_all(sends[0], "samp", 0, 0)]

    def collect(new_bf):
        if direct:
            return [new_bf] + swaps([new_bf] * (n_samp - 1), "samp")
        return [lax.all_gather(new_bf, "samp", axis=0, tiled=True)]

    def evaluate(halves, bases, adversary, step_q, step, keep, sent):
        sends = send_shapes(size * widths[0] + (2 * GRP if sent == BF16 else GRP), sent)
        own, loss, *rest = pl.pallas_call(
            functools.partial(grad_kernel, step, n_samp, row_blocks, bounds),
            out_shape=(
                blocks(size, widths[0], F32),
                shape((GRP, LANES), F32),
                *[blocks(slots, width, BF16) for width in widths[1:]],
                *sends,
            ),
            in_specs=[SM, SM, SM, SM] + [VM] * (5 + 2 * chunks),
            out_specs=(VM,) * (1 + chunks + len(sends)),
            scratch_shapes=[pltpu.VMEM((col_blocks, widths[0], block_size), F32)],
            compiler_params=PARAMS,
            cost_estimate=cost(work * widths[0], work),
            name="grad",
        )(me, slot_table, live, cols, x_data, label_rows, gid_rows, adversary, counts, *sum(halves, ()))
        if not flipped:
            flipped.append(flip(loss))
        rests, sends = rest[: chunks - 1], rest[chunks - 1 :]
        recvs = [exchange(sends)]
        owns = [own]
        for width, dz in zip(widths[1:], rests, strict=True):
            sends = send_shapes(size * width, sent)
            own, *sends = pl.pallas_call(
                functools.partial(more_grad_kernel, step, n_samp, row_blocks),
                out_shape=(blocks(size, width, F32), *sends),
                in_specs=[SM, SM, SM, VM, VM],
                out_specs=(VM,) * (1 + len(sends)),
                scratch_shapes=[pltpu.VMEM((col_blocks, width, block_size), F32)],
                compiler_params=PARAMS,
                cost_estimate=cost(work * width, work),
                name="more_grad",
            )(me, slot_table, cols, x_data, dz)
            owns.append(own)
            recvs.append(exchange(sends))
        news, logits = [], []
        for h, width in enumerate(widths):
            outs = (blocks(size, width, BF16),) + ((blocks(size, width, F32),) if keep else ())
            count = len(recvs[h])
            if h == 0:
                new_q, new_bf, *new = pl.pallas_call(
                    functools.partial(update_kernel, step, rate, keep, count),
                    out_shape=(shape((GRP, LANES), F32), *outs),
                    in_specs=[SM] + [VM] * (5 + count),
                    out_specs=(VM,) * (1 + len(outs)),
                    compiler_params=PARAMS,
                    name="update",
                )(me, owns[h], bases[h], loss, step_q, counts, *recvs[h][::-1])
            else:
                new_bf, *new = pl.pallas_call(
                    functools.partial(more_update_kernel, rate, keep, count),
                    out_shape=outs,
                    in_specs=[SM] + [VM] * (2 + count),
                    out_specs=(VM,) * len(outs),
                    compiler_params=PARAMS,
                    name="more_update",
                )(me, owns[h], bases[h], *recvs[h][::-1])
            news += new
            logits.append(collect(new_bf))
        return news, logits, new_q

    def halves_of(parts, step):
        return [feat_halves(forward(part, step, width)[0]) for part, width in zip(parts, widths, strict=True)]

    flipped = []
    adversary = jnp.full((GRP, LANES), 1.0 / GRP, F32)
    halves = [feat_halves(partial) for partial in partials]
    for step in range(STEPS):
        _, parts, half_q = evaluate(halves, states, adversary, adversary, step, False, BF16 if step else F32)
        halves = halves_of(parts, step)
        states_new, parts, adversary = evaluate(halves, states, half_q, adversary, step, step + 1 < STEPS, BF16)
        if step + 1 < STEPS:
            states = states_new
            halves = halves_of(parts, step + 1)
    mine, give = forward(parts[0], None, classes)
    mine, mask = mine + swap(give, "feat", 1), 2
    while mask < n_feat:
        mine = mine + swap(mine, "feat", mask)
        mask *= 2
    scores = pl.pallas_call(
        scores_kernel,
        out_shape=shape((classes, row_blocks * block_size), F32),
        in_specs=[SM, VM, VM],
        out_specs=VM,
        compiler_params=PARAMS,
        name="scores",
    )(me, mine, swap(mine, "feat", 1))
    return (scores.T, adversary[:, 0])


def solution(mesh):
    in_specs = (
        P(("groups", "samp"), "feat", None, None),
        P("groups", "feat"),
        P("groups"),
        P("groups"),
        P(None, "groups"),
        P("feat", None),
    )
    out_specs = (P(("groups", "samp"), None), P("groups"))
    return jax.shard_map(
        per_device, mesh=mesh, in_specs=in_specs, out_specs=out_specs, check_vma=False
    )
```
